512 devices in a mesh: grp: 16 (over y, x_hi), blk: 32 (over x_lo, z, core).
Axes of the slice: x: 4 (x_hi: 2, x_lo: 2; x = x_hi * 2 + x_lo), y: 8, z: 8, core: 2. Of those that a mesh axis runs over, the one named last changes fastest.
Arguments:
- sigma_anc: float32 [16384, 16384], P('grp', 'blk')
- panels: float32 [16384, 1024], P(('grp', 'blk')), may hold values from -0.0625 to 0.0625
- diag_inv: float32 [1024, 256], replicated, may hold values from -6 to 6
- scaled_parent_panel: float32 [512, 256], replicated, may hold values from -0.375 to 0.375
- struct_upper: int32 [2, 32], replicated, may hold values from 0 to 63, as said below
- struct_lower: int32 [2, 16], replicated, may hold values from 0 to 63, as said below
Outputs:
- cov_panel: float32 [16384, 1024], P(('blk', 'grp'))
- cov_diag: float32 [1024, 256], P('blk')
- cov_parent: float32 [512, 256], P('blk')
The draws below stay inside these ranges and needn't reach their ends.
Inputs may be any that keep to these rules, and one draw needn't show every extreme that they name: `struct_upper`: each row lists 32 different ancestor blocks. `struct_lower`: each row lists 16 different blocks, all in its parent's row of struct_upper.
All inputs are finite; a program needn't handle non-finite values.
Results may differ from the reference program's by a relative error of at most 0.00011.
Values sent between devices are 32-bit elements; how exact they have to be, the bound alone decides.
A program may use at most 64 MiB of HBM per device.

```python
import math
import jax
import jax.numpy as jnp
from jax import lax

NODE_WIDTH = 256
UPPER_NODES_1 = 2
LOWER_NODES_2 = 2
NS = 4
ANCESTOR_COLUMNS = 16384
NA = 64
K1 = 32
K2 = 16


def structure_all(key):
    keys_up = jax.random.split(jax.random.fold_in(key, 11), UPPER_NODES_1)
    lists_up = jax.vmap(lambda k: jax.random.permutation(k, NA)[:K1])(keys_up).astype(jnp.int32)
    parent_ids = (jnp.arange(LOWER_NODES_2, dtype=jnp.int32) % UPPER_NODES_1).astype(jnp.int32)
    keys_low = jax.random.split(jax.random.fold_in(key, 13), LOWER_NODES_2)
    picks = jax.vmap(lambda k: jax.random.permutation(k, K1)[:K2])(keys_low).astype(jnp.int32)
    lists_low = jnp.take_along_axis(lists_up[parent_ids], picks, axis=1).astype(jnp.int32)
    return (lists_up, lists_low)


def draw_struct_upper(key, part):
    return structure_all(key)[0]


def draw_struct_lower(key, part):
    return structure_all(key)[1]


def draw_sigma_anc(key, part):
    base = jax.random.normal(key, (ANCESTOR_COLUMNS, ANCESTOR_COLUMNS), jnp.float32)
    sym = (base + base.T) * math.sqrt(0.5)
    return sym.astype(jnp.float32)


def block_levels(rng, shape, cuts, low, top_value):
    def one(position, blocks):
        steps = jax.random.uniform(jax.random.fold_in(jax.random.fold_in(rng, 6), position), (blocks,), jnp.float32, low / len(cuts), top_value / len(cuts))
        return jnp.repeat(jnp.exp(steps), shape[position] // blocks).reshape((-1,) + (1,) * (len(shape) - position - 1))

    factor_of = one(*cuts[0])
    for cut in cuts[1:]:
        factor_of = factor_of * one(*cut)
    return factor_of


def scatter_about(stream_key, dims, deviation, reach, cuts=(), held_as=jnp.bfloat16):
    array = jax.random.normal(stream_key, dims, jnp.float32) * deviation
    if len(cuts) > 0:
        array = block_levels(stream_key, dims, cuts, -0.22, 0.18) * array
    return jnp.clip(array, min=-reach, max=reach).astype(held_as)


def setup_inputs(seed: int = 0) -> dict:
    keys = jax.random.split(jax.random.key(seed), 7)
    return {
        "sigma_anc": draw_sigma_anc(jax.random.fold_in(keys[6], 71), 0),
        "panels": scatter_about(keys[1], (ANCESTOR_COLUMNS, NS * NODE_WIDTH), (K1 * NODE_WIDTH) ** -0.5, 0.0625, ((0, 512),), jnp.float32),
        "diag_inv": scatter_about(keys[2], (NS * NODE_WIDTH, NODE_WIDTH), 1.0, 6.0, (), jnp.float32),
        "scaled_parent_panel": scatter_about(keys[3], (LOWER_NODES_2 * NODE_WIDTH, NODE_WIDTH), NODE_WIDTH ** -0.5, 0.375, (), jnp.float32),
        "struct_upper": draw_struct_upper(jax.random.fold_in(keys[6], 71), 0),
        "struct_lower": draw_struct_lower(jax.random.fold_in(keys[6], 71), 0),
    }


HIGH_ACCURACY = lax.Precision.HIGHEST


def block_table(struct_upper, struct_lower):
    ids = jnp.arange(NA, dtype=jnp.int32)
    upper = jnp.any(struct_upper[:, :, None] == ids[None, None, :], axis=1)
    lower = jnp.any(struct_lower[:, :, None] == ids[None, None, :], axis=1)
    return jnp.concatenate([upper, lower], axis=0).astype(jnp.float32)


def reference(sigma_anc, panels, diag_inv, scaled_parent_panel, struct_upper, struct_lower):
    table = block_table(struct_upper, struct_lower)
    rows_mask = jnp.repeat(table.T, NODE_WIDTH, axis=0)
    matrix_columns = jnp.repeat(rows_mask, NODE_WIDTH, axis=1)
    upanel = panels * matrix_columns
    inverse_complete = jnp.dot(sigma_anc, upanel, precision=HIGH_ACCURACY, preferred_element_type=jnp.float32)
    upper_width_1 = UPPER_NODES_1 * NODE_WIDTH
    g_up = -(matrix_columns[:, :upper_width_1] * inverse_complete[:, :upper_width_1])
    parent_ids = jnp.arange(LOWER_NODES_2, dtype=jnp.int32) % UPPER_NODES_1
    membership_grid = (parent_ids[:, None] == jnp.arange(UPPER_NODES_1, dtype=jnp.int32)[None, :]).astype(jnp.float32)
    collected_elder_share = jnp.einsum('rjw,cj->rcw', g_up.reshape(ANCESTOR_COLUMNS, UPPER_NODES_1, NODE_WIDTH), membership_grid, precision=HIGH_ACCURACY)
    stacked_arrays = scaled_parent_panel.reshape(LOWER_NODES_2, NODE_WIDTH, NODE_WIDTH)
    resolved_bottom_share = matrix_columns[:, upper_width_1:].reshape(ANCESTOR_COLUMNS, LOWER_NODES_2, NODE_WIDTH) * (jnp.einsum('odf,dfy->ody', collected_elder_share, stacked_arrays, precision=HIGH_ACCURACY) + inverse_complete[:, upper_width_1:].reshape(ANCESTOR_COLUMNS, LOWER_NODES_2, NODE_WIDTH))
    cov_panel = jnp.concatenate([g_up, -resolved_bottom_share.reshape(ANCESTOR_COLUMNS, LOWER_NODES_2 * NODE_WIDTH)], axis=1)
    u_up = upanel[:, :upper_width_1].reshape(ANCESTOR_COLUMNS, UPPER_NODES_1, NODE_WIDTH)
    u_low = upanel[:, upper_width_1:].reshape(ANCESTOR_COLUMNS, LOWER_NODES_2, NODE_WIDTH)
    amat = jnp.einsum('rjw,rjv->jwv', u_up, inverse_complete[:, :upper_width_1].reshape(ANCESTOR_COLUMNS, UPPER_NODES_1, NODE_WIDTH), precision=HIGH_ACCURACY)
    block_matrix = jnp.einsum('rcw,rcv->cwv', u_low, collected_elder_share, precision=HIGH_ACCURACY)
    extra_matrix = jnp.einsum('rcw,rcv->cwv', u_low, resolved_bottom_share, precision=HIGH_ACCURACY)
    diagonal_matrices = diag_inv.reshape(UPPER_NODES_1 + LOWER_NODES_2, NODE_WIDTH, NODE_WIDTH)
    s_up = diagonal_matrices[:UPPER_NODES_1] + amat
    parent_selection = jnp.einsum('cj,jwv->cwv', membership_grid, s_up, precision=HIGH_ACCURACY)
    solved_parent = jnp.einsum('ghz,gzs->ghs', parent_selection, stacked_arrays, precision=HIGH_ACCURACY) + jnp.transpose(block_matrix, (0, 2, 1))
    lower_selection = diagonal_matrices[UPPER_NODES_1:] + jnp.einsum('lmt,lmx->ltx', stacked_arrays, solved_parent, precision=HIGH_ACCURACY) + extra_matrix
    cov_diag = jnp.concatenate([s_up, lower_selection], axis=0).reshape((UPPER_NODES_1 + LOWER_NODES_2) * NODE_WIDTH, NODE_WIDTH)
    cov_parent = -solved_parent.reshape(LOWER_NODES_2 * NODE_WIDTH, NODE_WIDTH)
    return cov_panel, cov_diag, cov_parent
```

```python
import jax
import jax.numpy as jnp
from jax import lax
from jax.sharding import PartitionSpec as P

W = 256
HIGH = lax.Precision.HIGH
HIGHEST = lax.Precision.HIGHEST


def dot(a, b, ca, cb, precision=HIGH):
    return lax.dot_general(
        a, b, (((ca,), (cb,)), ((), ())), precision=precision, preferred_element_type=jnp.float32
    )


def listed(struct_upper, struct_lower, block):
    upper = jnp.any(struct_upper == block, axis=1)
    lower = jnp.any(struct_lower == block, axis=1)
    flags = jnp.concatenate([upper, lower]).astype(jnp.float32)
    return jnp.repeat(flags, W)[None, :]


def gather_rows(rows):
    return lax.all_gather(rows, "blk", axis=0, tiled=True)


def scatter_products(partial):
    return lax.psum_scatter(partial, "grp", scatter_dimension=0, tiled=True)


def sum_blocks(terms):
    return lax.psum(lax.psum_scatter(terms, "blk", scatter_dimension=0, tiled=True), "grp")


def per_device(sigma_anc, panels, diag_inv, scaled_parent_panel, struct_upper, struct_lower):
    grp = lax.axis_index("grp")
    blk = lax.axis_index("blk")
    v = [scaled_parent_panel[:W], scaled_parent_panel[W:]]
    u = panels * listed(struct_upper, struct_lower, (grp * 32 + blk) // 8)
    x = [dot(u[:, c * W : (c + 1) * W], v[c], 1, 0) - u[:, (c + 2) * W : (c + 3) * W] for c in (0, 1)]
    w = jnp.concatenate([u[:, : 2 * W], x[0], x[1]], axis=1)
    moves = [(q, (q % 16) * 32 + q // 16) for q in range(512)]
    w_own = lax.ppermute(w, ("grp", "blk"), moves)
    gathered = gather_rows(w)
    t = scatter_products(dot(sigma_anc, gathered, 0, 0))
    own = listed(struct_upper, struct_lower, (blk * 16 + grp) // 8)
    sign = jnp.where(jnp.arange(4 * W) < 2 * W, -1.0, 1.0).astype(jnp.float32)[None, :]
    cov_panel = t * (own * sign)

    def part(a, i):
        return a[:, i * W : (i + 1) * W]

    diag_terms = [dot(part(w_own, i), part(t, i), 0, 0) for i in range(4)]
    parent_terms = [dot(part(w_own, c), part(t, c + 2), 0, 0) for c in (0, 1)]
    terms = jnp.concatenate(
        [
            jnp.concatenate(diag_terms, axis=0).reshape(32, 32, W),
            jnp.concatenate(parent_terms, axis=0).reshape(32, 16, W),
        ],
        axis=1,
    ).reshape(32 * 48, W)
    base_parent = [dot(diag_inv[c * W : (c + 1) * W], v[c], 1, 0, HIGHEST) for c in (0, 1)]
    base_low = [dot(v[c], base_parent[c], 0, 0, HIGHEST) for c in (0, 1)]
    zero = jnp.zeros((2 * W, W), jnp.float32)
    base_diag = diag_inv + jnp.concatenate([zero] + base_low, axis=0)
    base_parent = jnp.concatenate(base_parent, axis=0)
    summed = sum_blocks(terms)
    cov_diag = lax.dynamic_slice_in_dim(base_diag, blk * 32, 32, 0) + summed[:32]
    cov_parent = -(lax.dynamic_slice_in_dim(base_parent, blk * 16, 16, 0) + summed[32:])
    return (cov_panel, cov_diag, cov_parent)


def solution(mesh):
    return jax.shard_map(
        per_device,
        mesh=mesh,
        in_specs=(P("grp", "blk"), P(("grp", "blk"), None), P(), P(), P(), P()),
        out_specs=(P(("blk", "grp"), None), P("blk", None), P("blk", None)),
        check_vma=False,
    )
```

```python
import jax
import jax.numpy as jnp
from jax import lax
from jax.experimental import pallas as pl
from jax.experimental.pallas import tpu as pltpu
from jax.sharding import PartitionSpec as P

W = 256
HIGH = lax.Precision.HIGH
HIGHEST = lax.Precision.HIGHEST


def dot(a, b, ca, cb, precision=HIGH):
    return lax.dot_general(
        a, b, (((ca,), (cb,)), ((), ())), precision=precision, preferred_element_type=jnp.float32
    )


def listed(struct_upper, struct_lower, block):
    upper = jnp.any(struct_upper == block, axis=1)
    lower = jnp.any(struct_lower == block, axis=1)
    flags = jnp.concatenate([upper, lower]).astype(jnp.float32)
    return jnp.repeat(flags, W)[None, :]


VMEM = pl.BlockSpec(memory_space=pltpu.VMEM)
DMA = pltpu.SemaphoreType.DMA


def greet(axes_and_peers):
    barrier = pltpu.get_barrier_semaphore()
    for axis, peer in axes_and_peers:
        pl.semaphore_signal(
            barrier, inc=1, device_id={axis: peer}, device_id_type=pl.DeviceIdType.MESH
        )
    pl.semaphore_wait(barrier, len(axes_and_peers))


def send(src, dst, send_sem, recv_sem, axis, peer):
    copy = pltpu.make_async_remote_copy(
        src_ref=src,
        dst_ref=dst,
        send_sem=send_sem,
        recv_sem=recv_sem,
        device_id={axis: peer},
        device_id_type=pl.DeviceIdType.MESH,
    )
    copy.start()
    return copy


def call(kernel, out_shape, scratch, collective_id, operand, sent):
    return pl.pallas_call(
        kernel,
        out_shape=jax.ShapeDtypeStruct(out_shape, jnp.float32),
        in_specs=[VMEM],
        out_specs=VMEM,
        scratch_shapes=scratch,
        cost_estimate=pl.CostEstimate(flops=1000000, bytes_accessed=sent, transcendentals=0),
        compiler_params=pltpu.CompilerParams(
            collective_id=collective_id, has_side_effects=True, vmem_limit_bytes=40 * 2**20
        ),
    )(operand)


def gather_kernel(w_ref, o_ref, z_send, z_recv, x_send, x_recv, c_send, c_recv):
    b = lax.axis_index("blk")
    core, z, xl = b % 2, (b // 2) % 8, b // 16
    across, sibling = (1 - xl) * 16 + z * 2 + core, xl * 16 + z * 2 + 1 - core
    ring = [xl * 16 + ((z + 1) % 8) * 2 + core, xl * 16 + ((z + 7) % 8) * 2 + core]
    greet([("blk", p) for p in ring + [across, sibling]])
    copies = []
    x_copy = send(w_ref, o_ref.at[xl, z, core], x_send, x_recv, "blk", across)

    def share(src, dst, e, i):
        copies.append(send(src, dst, c_send.at[e, i], c_recv.at[e, i], "blk", sibling))

    hops = [[4, 3], [3, 4]]
    travelling = {}
    for s in range(5):
        for e in range(2):
            x = xl if e == 0 else 1 - xl
            if s == 0:
                if e == 1:
                    x_copy.wait()
                here = o_ref.at[x, z, core]
                src = w_ref if e == 0 else here
                for d in range(2):
                    travelling[e, d] = send(
                        src, here, z_send.at[e, d, 0], z_recv.at[e, d, 0], "blk", ring[d]
                    )
                share(src, here, e, 0)
                continue
            for d in range(2):
                if s > hops[e][d]:
                    continue
                origin = (z + (8 - s)) % 8 if d == 0 else (z + s) % 8
                here = o_ref.at[x, origin, core]
                travelling[e, d].wait_recv()
                copies_done = travelling[e, d]
                copies.append((copies_done,))
                if s < hops[e][d]:
                    travelling[e, d] = send(
                        here, here, z_send.at[e, d, s], z_recv.at[e, d, s], "blk", ring[d]
                    )
                share(here, here, e, 4 * d + s)
    o_ref[xl, z, core] = w_ref[...]
    for copy in copies:
        if isinstance(copy, tuple):
            copy[0].wait_send()
        else:
            copy.wait()


def gather_rows(rows):
    scratch = [DMA((2, 2, 4)), DMA((2, 2, 4)), DMA, DMA, DMA((2, 9)), DMA((2, 9))]
    out = call(gather_kernel, (2, 8, 2, 32, 4 * W), scratch, 1, rows, 2**22)
    return out.reshape(1024, 4 * W)


def scatter_kernel(p_ref, o_ref, held, final, y_send, y_recv, x_send, x_recv):
    g = lax.axis_index("grp")
    y, h = g // 2, g % 2
    ring = [((y + 1) % 8) * 2 + h, ((y + 7) % 8) * 2 + h]
    across = y * 2 + 1 - h
    greet([("grp", p) for p in ring + [across]])
    copies = {}
    for s in range(8):
        for q in range(4):
            columns = pl.ds(q * W, W)
            chunk = (y + (7 - s)) % 8 if q % 2 == 0 else (y + 1 + s) % 8
            rows = pl.ds(pl.multiple_of(chunk * 64, 64), 64)
            if s == 0:
                src = p_ref.at[rows, columns]
            else:
                copies[s - 1, q].wait_recv()
                held[s - 1, q] = held[s - 1, q] + p_ref[rows, columns]
                src = held.at[s - 1, q]
            if s < 7:
                copies[s, q] = send(
                    src, held.at[s, q], y_send.at[s, q], y_recv.at[s, q], "grp", ring[q % 2]
                )
            else:
                theirs = pl.ds(pl.multiple_of((1 - h) * 32, 32), 32)
                copies[s, q] = send(
                    held.at[6, q, theirs], final.at[q], x_send.at[q], x_recv.at[q], "grp", across
                )
    mine = pl.ds(pl.multiple_of(h * 32, 32), 32)
    for q in range(4):
        copies[7, q].wait_recv()
        o_ref[:, q * W : (q + 1) * W] = held[6, q, mine] + final[q]
    for copy in copies.values():
        copy.wait_send()


def scatter_products(partial):
    scratch = [
        pltpu.VMEM((7, 4, 64, W), jnp.float32),
        pltpu.VMEM((4, 32, W), jnp.float32),
        DMA((7, 4)),
        DMA((7, 4)),
        DMA((4,)),
        DMA((4,)),
    ]
    return call(scatter_kernel, (32, 4 * W), scratch, 2, partial, 2**22)


def sum_kernel(t_ref, o_ref, pair, z_held, total, x_held, part, h_held, y_held, s_sem, r_sem):
    g, b = lax.axis_index("grp"), lax.axis_index("blk")
    y, h = g // 2, g % 2
    core, z, xl = b % 2, (b // 2) % 8, b // 16
    far_first = (4, 3, 5, 2, 6, 1, 7)
    sibling, across = xl * 16 + z * 2 + 1 - core, (1 - xl) * 16 + z * 2 + core
    z_peers = {d: xl * 16 + ((z + d) % 8) * 2 + core for d in far_first}
    y_peers = {d: ((y + d) % 8) * 2 + h for d in far_first}
    other = y * 2 + 1 - h
    greet(
        [("blk", sibling), ("blk", across), ("grp", other)]
        + [("blk", z_peers[d]) for d in far_first]
        + [("grp", y_peers[d]) for d in far_first]
    )
    copies = []

    def pass_on(src, dst, i, axis, peer):
        copies.append(send(src, dst, s_sem.at[i], r_sem.at[i], axis, peer))
        return copies[-1]

    first = {}
    for d in far_first + (8,):
        k = (z + d) % 8
        first[d] = pass_on(t_ref.at[k, 1 - core], pair.at[k], 8 + d, "blk", sibling)
    second = {}
    for d in far_first:
        k = (z + d) % 8
        first[d].wait_recv()
        pair[k] = pair[k] + t_ref[k, core]
        second[d] = pass_on(pair.at[k], z_held.at[d - 1], d, "blk", z_peers[d])
    first[8].wait_recv()
    total[...] = pair[z] + t_ref[z, core]
    for d in reversed(far_first):
        second[d].wait_recv()
        total[...] = total[...] + z_held[d - 1]
    pass_on(total.at[1 - xl], x_held, 17, "blk", across).wait_recv()
    part[...] = total[xl] + x_held[...]
    pass_on(part, h_held, 18, "grp", other).wait_recv()
    y_held[y] = part[...] + h_held[...]
    third = [pass_on(y_held.at[y], y_held.at[y], 18 + d, "grp", y_peers[d]) for d in far_first]
    for copy in third:
        copy.wait_recv()
    result = y_held[0]
    for k in range(1, 8):
        result = result + y_held[k]
    o_ref[...] = result
    for copy in copies:
        copy.wait_send()


def sum_blocks(terms):
    terms = terms.reshape(2, 8, 2, 48, W).transpose(1, 2, 0, 3, 4)
    scratch = [
        pltpu.VMEM((8, 2, 48, W), jnp.float32),
        pltpu.VMEM((7, 2, 48, W), jnp.float32),
        pltpu.VMEM((2, 48, W), jnp.float32),
        pltpu.VMEM((48, W), jnp.float32),
        pltpu.VMEM((48, W), jnp.float32),
        pltpu.VMEM((48, W), jnp.float32),
        pltpu.VMEM((8, 48, W), jnp.float32),
        DMA((26,)),
        DMA((26,)),
    ]
    return call(sum_kernel, (48, W), scratch, 3, terms, 2**22)


def per_device(sigma_anc, panels, diag_inv, scaled_parent_panel, struct_upper, struct_lower):
    grp = lax.axis_index("grp")
    blk = lax.axis_index("blk")
    v = [scaled_parent_panel[:W], scaled_parent_panel[W:]]
    u = panels * listed(struct_upper, struct_lower, (grp * 32 + blk) // 8)
    x = [dot(u[:, c * W : (c + 1) * W], v[c], 1, 0) - u[:, (c + 2) * W : (c + 3) * W] for c in (0, 1)]
    w = jnp.concatenate([u[:, : 2 * W], x[0], x[1]], axis=1)
    moves = [(q, (q % 16) * 32 + q // 16) for q in range(512)]
    w_own = lax.ppermute(w, ("grp", "blk"), moves)
    gathered = gather_rows(w)
    t = scatter_products(dot(sigma_anc, gathered, 0, 0))
    own = listed(struct_upper, struct_lower, (blk * 16 + grp) // 8)
    sign = jnp.where(jnp.arange(4 * W) < 2 * W, -1.0, 1.0).astype(jnp.float32)[None, :]
    cov_panel = t * (own * sign)

    def part(a, i):
        return a[:, i * W : (i + 1) * W]

    diag_terms = [dot(part(w_own, i), part(t, i), 0, 0) for i in range(4)]
    parent_terms = [dot(part(w_own, c), part(t, c + 2), 0, 0) for c in (0, 1)]
    terms = jnp.concatenate(
        [
            jnp.concatenate(diag_terms, axis=0).reshape(32, 32, W),
            jnp.concatenate(parent_terms, axis=0).reshape(32, 16, W),
        ],
        axis=1,
    ).reshape(32 * 48, W)
    base_parent = [dot(diag_inv[c * W : (c + 1) * W], v[c], 1, 0, HIGHEST) for c in (0, 1)]
    base_low = [dot(v[c], base_parent[c], 0, 0, HIGHEST) for c in (0, 1)]
    zero = jnp.zeros((2 * W, W), jnp.float32)
    base_diag = diag_inv + jnp.concatenate([zero] + base_low, axis=0)
    base_parent = jnp.concatenate(base_parent, axis=0)
    summed = sum_blocks(terms)
    cov_diag = lax.dynamic_slice_in_dim(base_diag, blk * 32, 32, 0) + summed[:32]
    cov_parent = -(lax.dynamic_slice_in_dim(base_parent, blk * 16, 16, 0) + summed[32:])
    return (cov_panel, cov_diag, cov_parent)


def solution(mesh):
    return jax.shard_map(
        per_device,
        mesh=mesh,
        in_specs=(P("grp", "blk"), P(("grp", "blk"), None), P(), P(), P(), P()),
        out_specs=(P(("blk", "grp"), None), P("blk", None), P("blk", None)),
        check_vma=False,
    )
```

```python
import jax
import jax.numpy as jnp
from jax import lax
from jax.experimental import pallas as pl
from jax.experimental.pallas import tpu as pltpu
from jax.sharding import PartitionSpec as P

W = 256
HIGH = lax.Precision.HIGH
HIGHEST = lax.Precision.HIGHEST


def dot(a, b, ca, cb, precision=HIGH):
    return lax.dot_general(
        a, b, (((ca,), (cb,)), ((), ())), precision=precision, preferred_element_type=jnp.float32
    )


def listed(struct_upper, struct_lower, block):
    upper = jnp.any(struct_upper == block, axis=1)
    lower = jnp.any(struct_lower == block, axis=1)
    flags = jnp.concatenate([upper, lower]).astype(jnp.float32)
    return jnp.repeat(flags, W)[None, :]


VMEM = pl.BlockSpec(memory_space=pltpu.VMEM)
DMA = pltpu.SemaphoreType.DMA


def greet(axes_and_peers):
    barrier = pltpu.get_barrier_semaphore()
    for axis, peer in axes_and_peers:
        pl.semaphore_signal(
            barrier, inc=1, device_id={axis: peer}, device_id_type=pl.DeviceIdType.MESH
        )
    pl.semaphore_wait(barrier, len(axes_and_peers))


def send(src, dst, send_sem, recv_sem, axis, peer):
    copy = pltpu.make_async_remote_copy(
        src_ref=src,
        dst_ref=dst,
        send_sem=send_sem,
        recv_sem=recv_sem,
        device_id={axis: peer},
        device_id_type=pl.DeviceIdType.MESH,
    )
    copy.start()
    return copy


def call(kernel, out_shape, scratch, collective_id, operands, sent):
    return pl.pallas_call(
        kernel,
        out_shape=jax.ShapeDtypeStruct(out_shape, jnp.float32),
        in_specs=[VMEM] * len(operands),
        out_specs=VMEM,
        scratch_shapes=scratch,
        cost_estimate=pl.CostEstimate(flops=1000000, bytes_accessed=sent, transcendentals=0),
        compiler_params=pltpu.CompilerParams(
            collective_id=collective_id, has_side_effects=True, vmem_limit_bytes=40 * 2**20
        ),
    )(*operands)


def gather_steps(w_ref, o_ref, columns, ids, z_send, z_recv, x_send, x_recv, c_send, c_recv):
    core, z, xl = ids
    across, sibling = (1 - xl) * 16 + z * 2 + core, xl * 16 + z * 2 + 1 - core
    ring = [xl * 16 + ((z + 1) % 8) * 2 + core, xl * 16 + ((z + 7) % 8) * 2 + core]
    own = w_ref.at[:, columns]
    arriving, leaving = [], []
    x_copy = send(own, o_ref.at[xl, z, core], x_send, x_recv, "blk", across)

    def share(src, dst, e, i):
        arriving.append(send(src, dst, c_send.at[e, i], c_recv.at[e, i], "blk", sibling))

    hops = [[4, 3], [3, 4]]
    travelling = {}
    for s in range(5):
        for e in range(2):
            x = xl if e == 0 else 1 - xl
            if s == 0:
                if e == 1:
                    yield
                    x_copy.wait()
                here = o_ref.at[x, z, core]
                src = own if e == 0 else here
                for d in range(2):
                    travelling[e, d] = send(
                        src, here, z_send.at[e, d, 0], z_recv.at[e, d, 0], "blk", ring[d]
                    )
                    leaving.append(travelling[e, d])
                share(src, here, e, 0)
                continue
            for d in range(2):
                if s > hops[e][d]:
                    continue
                origin = (z + (8 - s)) % 8 if d == 0 else (z + s) % 8
                here = o_ref.at[x, origin, core]
                travelling[e, d].wait_recv()
                if s < hops[e][d]:
                    travelling[e, d] = send(
                        here, here, z_send.at[e, d, s], z_recv.at[e, d, s], "blk", ring[d]
                    )
                    leaving.append(travelling[e, d])
                share(here, here, e, 4 * d + s)
        yield
    o_ref[xl, z, core] = w_ref[:, columns]
    for copy in leaving:
        copy.wait_send()
    for copy in arriving:
        copy.wait()


def scatter_steps(p_ref, o_ref, first, held, final, ids, y_send, y_recv, x_send, x_recv):
    y, h = ids
    ring = [((y + 1) % 8) * 2 + h, ((y + 7) % 8) * 2 + h]
    across = y * 2 + 1 - h
    width = W // 2
    copies = {}
    for s in range(8):
        for q in range(4):
            columns = pl.ds(q * width, width)
            chunk = (y + (7 - s)) % 8 if q % 2 == 0 else (y + 1 + s) % 8
            if s == 0:
                src = p_ref.at[chunk, :, columns]
            else:
                copies[s - 1, q].wait_recv()
                held[s - 1, q] = held[s - 1, q] + p_ref[chunk, :, columns]
                src = held.at[s - 1, q]
            if s < 7:
                copies[s, q] = send(
                    src, held.at[s, q], y_send.at[s, q], y_recv.at[s, q], "grp", ring[q % 2]
                )
            else:
                theirs = pl.ds(pl.multiple_of((1 - h) * 32, 32), 32)
                copies[s, q] = send(
                    held.at[6, q, theirs], final.at[q], x_send.at[q], x_recv.at[q], "grp", across
                )
        yield
    mine = pl.ds(pl.multiple_of(h * 32, 32), 32)
    for q in range(4):
        copies[7, q].wait_recv()
        o_ref[:, first + q * width : first + (q + 1) * width] = held[6, q, mine] + final[q]
    for copy in copies.values():
        copy.wait_send()


def split(value):
    high = value.astype(jnp.bfloat16)
    return high, (value - high.astype(jnp.float32)).astype(jnp.bfloat16)


def product_kernel(
    s_ref, w_ref, o_ref, rows, s_high, s_low, r_high, r_low, partial, held, final, *sems
):
    g, b = lax.axis_index("grp"), lax.axis_index("blk")
    y, h = g // 2, g % 2
    core, z, xl = b % 2, (b // 2) % 8, b // 16
    greet(
        [
            ("blk", xl * 16 + ((z + 1) % 8) * 2 + core),
            ("blk", xl * 16 + ((z + 7) % 8) * 2 + core),
            ("blk", (1 - xl) * 16 + z * 2 + core),
            ("blk", xl * 16 + z * 2 + 1 - core),
            ("grp", ((y + 1) % 8) * 2 + h),
            ("grp", ((y + 7) % 8) * 2 + h),
            ("grp", y * 2 + 1 - h),
        ]
    )
    g_sems, y_sems = sems[:6], sems[6:]

    def at(refs, half):
        return [ref.at[half] for ref in refs]

    gathers = [
        gather_steps(
            w_ref, rows.at[i], pl.ds(i * 2 * W, 2 * W), (core, z, xl), *at(g_sems, i)
        )
        for i in range(2)
    ]
    scatters = [
        scatter_steps(
            partial.at[i], o_ref, i * 2 * W, held.at[i], final.at[i], (y, h), *at(y_sems, i)
        )
        for i in range(2)
    ]

    def product(half):
        high, low = split(rows[half].reshape(1024, 2 * W))
        r_high[...] = high
        r_low[...] = low

        @pl.loop(0, 4)
        def _(m):
            some = pl.ds(pl.multiple_of(m * 128, 128), 128)

            def mul(p, q):
                return jnp.dot(p[some, :], q[...], preferred_element_type=jnp.float32)

            total = mul(s_high, r_low) + mul(s_low, r_high) + mul(s_high, r_high)
            partial[half, pl.ds(m * 2, 2)] = total.reshape(2, 64, 2 * W)

    def step(steps):
        next(steps, None)

    step(gathers[0])
    for i in range(8):
        some = slice(i * 128, (i + 1) * 128)
        s_high[:, some], s_low[:, some] = split(s_ref[some, :].T)
    for _ in range(4):
        step(gathers[0])
    step(gathers[1])
    step(gathers[0])
    step(gathers[1])
    step(gathers[0])
    product(0)
    step(scatters[0])
    for _ in range(5):
        step(gathers[1])
        step(scatters[0])
    product(1)
    for _ in range(9):
        step(scatters[1])
        step(scatters[0])


def products(sigma, rows):
    f32, bf16 = jnp.float32, jnp.bfloat16
    scratch = [
        pltpu.VMEM((2, 2, 8, 2, 32, 2 * W), f32),
        pltpu.VMEM((512, 1024), bf16),
        pltpu.VMEM((512, 1024), bf16),
        pltpu.VMEM((1024, 2 * W), bf16),
        pltpu.VMEM((1024, 2 * W), bf16),
        pltpu.VMEM((2, 8, 64, 2 * W), f32),
        pltpu.VMEM((2, 7, 4, 64, W // 2), f32),
        pltpu.VMEM((2, 4, 32, W // 2), f32),
        DMA((2, 2, 2, 4)),
        DMA((2, 2, 2, 4)),
        DMA((2,)),
        DMA((2,)),
        DMA((2, 2, 9)),
        DMA((2, 2, 9)),
        DMA((2, 7, 4)),
        DMA((2, 7, 4)),
        DMA((2, 4)),
        DMA((2, 4)),
    ]
    return call(product_kernel, (32, 4 * W), scratch, 1, [sigma, rows], 2**23)


def sum_kernel(t_ref, o_ref, pair, z_held, total, x_held, part, h_held, y_held, s_sem, r_sem):
    g, b = lax.axis_index("grp"), lax.axis_index("blk")
    y, h = g // 2, g % 2
    core, z, xl = b % 2, (b // 2) % 8, b // 16
    far_first = (4, 3, 5, 2, 6, 1, 7)
    sibling, across = xl * 16 + z * 2 + 1 - core, (1 - xl) * 16 + z * 2 + core
    z_peers = {d: xl * 16 + ((z + d) % 8) * 2 + core for d in far_first}
    y_peers = {d: ((y + d) % 8) * 2 + h for d in far_first}
    other = y * 2 + 1 - h
    greet(
        [("blk", sibling), ("blk", across), ("grp", other)]
        + [("blk", z_peers[d]) for d in far_first]
        + [("grp", y_peers[d]) for d in far_first]
    )
    copies = []

    def pass_on(src, dst, i, axis, peer):
        copies.append(send(src, dst, s_sem.at[i], r_sem.at[i], axis, peer))
        return copies[-1]

    first = {}
    for d in far_first + (8,):
        k = (z + d) % 8
        first[d] = pass_on(t_ref.at[k, 1 - core], pair.at[k], 8 + d, "blk", sibling)
    second = {}
    for d in far_first:
        k = (z + d) % 8
        first[d].wait_recv()
        pair[k] = pair[k] + t_ref[k, core]
        second[d] = pass_on(pair.at[k], z_held.at[d - 1], d, "blk", z_peers[d])
    first[8].wait_recv()
    total[...] = pair[z] + t_ref[z, core]
    for d in reversed(far_first):
        second[d].wait_recv()
        total[...] = total[...] + z_held[d - 1]
    pass_on(total.at[1 - xl], x_held, 17, "blk", across).wait_recv()
    part[...] = total[xl] + x_held[...]
    pass_on(part, h_held, 18, "grp", other).wait_recv()
    y_held[y] = part[...] + h_held[...]
    third = [pass_on(y_held.at[y], y_held.at[y], 18 + d, "grp", y_peers[d]) for d in far_first]
    for copy in third:
        copy.wait_recv()
    result = y_held[0]
    for k in range(1, 8):
        result = result + y_held[k]
    o_ref[...] = result
    for copy in copies:
        copy.wait_send()


def sum_blocks(terms):
    terms = terms.reshape(2, 8, 2, 48, W).transpose(1, 2, 0, 3, 4)
    scratch = [
        pltpu.VMEM((8, 2, 48, W), jnp.float32),
        pltpu.VMEM((7, 2, 48, W), jnp.float32),
        pltpu.VMEM((2, 48, W), jnp.float32),
        pltpu.VMEM((48, W), jnp.float32),
        pltpu.VMEM((48, W), jnp.float32),
        pltpu.VMEM((48, W), jnp.float32),
        pltpu.VMEM((8, 48, W), jnp.float32),
        DMA((26,)),
        DMA((26,)),
    ]
    return call(sum_kernel, (48, W), scratch, 3, [terms], 2**22)


def per_device(sigma_anc, panels, diag_inv, scaled_parent_panel, struct_upper, struct_lower):
    grp = lax.axis_index("grp")
    blk = lax.axis_index("blk")
    v = [scaled_parent_panel[:W], scaled_parent_panel[W:]]
    u = panels * listed(struct_upper, struct_lower, (grp * 32 + blk) // 8)
    x = [dot(u[:, c * W : (c + 1) * W], v[c], 1, 0) - u[:, (c + 2) * W : (c + 3) * W] for c in (0, 1)]
    w = jnp.concatenate([u[:, : 2 * W], x[0], x[1]], axis=1)
    moves = [(q, (q % 16) * 32 + q // 16) for q in range(512)]
    w_own = lax.ppermute(w, ("grp", "blk"), moves)
    t = products(sigma_anc, w)
    own = listed(struct_upper, struct_lower, (blk * 16 + grp) // 8)
    sign = jnp.where(jnp.arange(4 * W) < 2 * W, -1.0, 1.0).astype(jnp.float32)[None, :]
    cov_panel = t * (own * sign)

    def part(a, i):
        return a[:, i * W : (i + 1) * W]

    diag_terms = [dot(part(w_own, i), part(t, i), 0, 0) for i in range(4)]
    parent_terms = [dot(part(w_own, c), part(t, c + 2), 0, 0) for c in (0, 1)]
    terms = jnp.concatenate(
        [
            jnp.concatenate(diag_terms, axis=0).reshape(32, 32, W),
            jnp.concatenate(parent_terms, axis=0).reshape(32, 16, W),
        ],
        axis=1,
    ).reshape(32 * 48, W)
    base_parent = [dot(diag_inv[c * W : (c + 1) * W], v[c], 1, 0, HIGHEST) for c in (0, 1)]
    base_low = [dot(v[c], base_parent[c], 0, 0, HIGHEST) for c in (0, 1)]
    zero = jnp.zeros((2 * W, W), jnp.float32)
    base_diag = diag_inv + jnp.concatenate([zero] + base_low, axis=0)
    base_parent = jnp.concatenate(base_parent, axis=0)
    summed = sum_blocks(terms)
    cov_diag = lax.dynamic_slice_in_dim(base_diag, blk * 32, 32, 0) + summed[:32]
    cov_parent = -(lax.dynamic_slice_in_dim(base_parent, blk * 16, 16, 0) + summed[32:])
    return (cov_panel, cov_diag, cov_parent)


def solution(mesh):
    return jax.shard_map(
        per_device,
        mesh=mesh,
        in_specs=(P("grp", "blk"), P(("grp", "blk"), None), P(), P(), P(), P()),
        out_specs=(P(("blk", "grp"), None), P("blk", None), P("blk", None)),
        check_vma=False,
    )
```

```python
import jax
import jax.numpy as jnp
from jax import lax
from jax.experimental import pallas as pl
from jax.experimental.pallas import tpu as pltpu
from jax.sharding import PartitionSpec as P

W = 256
HIGH = lax.Precision.HIGH
HIGHEST = lax.Precision.HIGHEST


def dot(a, b, ca, cb, precision=HIGH):
    return lax.dot_general(
        a, b, (((ca,), (cb,)), ((), ())), precision=precision, preferred_element_type=jnp.float32
    )


def listed(struct_upper, struct_lower, block):
    upper = jnp.any(struct_upper == block, axis=1)
    lower = jnp.any(struct_lower == block, axis=1)
    flags = jnp.concatenate([upper, lower]).astype(jnp.float32)
    return jnp.repeat(flags, W)[None, :]


VMEM = pl.BlockSpec(memory_space=pltpu.VMEM)
DMA = pltpu.SemaphoreType.DMA


def greet(axes_and_peers):
    barrier = pltpu.get_barrier_semaphore()
    for axis, peer in axes_and_peers:
        pl.semaphore_signal(
            barrier, inc=1, device_id={axis: peer}, device_id_type=pl.DeviceIdType.MESH
        )
    pl.semaphore_wait(barrier, len(axes_and_peers))


def send(src, dst, send_sem, recv_sem, axis, peer):
    copy = pltpu.make_async_remote_copy(
        src_ref=src,
        dst_ref=dst,
        send_sem=send_sem,
        recv_sem=recv_sem,
        device_id={axis: peer},
        device_id_type=pl.DeviceIdType.MESH,
    )
    copy.start()
    return copy


def call(kernel, out_shapes, scratch, collective_id, operands, sent):
    return pl.pallas_call(
        kernel,
        out_shape=[jax.ShapeDtypeStruct(shape, jnp.float32) for shape in out_shapes],
        in_specs=[VMEM] * len(operands),
        out_specs=[VMEM] * len(out_shapes),
        scratch_shapes=scratch,
        cost_estimate=pl.CostEstimate(flops=1000000, bytes_accessed=sent, transcendentals=0),
        compiler_params=pltpu.CompilerParams(
            collective_id=collective_id, has_side_effects=True, vmem_limit_bytes=40 * 2**20
        ),
    )(*operands)


def gather_kernel(w_ref, o_ref, z_send, z_recv, x_send, x_recv, c_send, c_recv):
    b = lax.axis_index("blk")
    core, z, xl = b % 2, (b // 2) % 8, b // 16
    across, sibling = (1 - xl) * 16 + z * 2 + core, xl * 16 + z * 2 + 1 - core
    ring = [xl * 16 + ((z + 1) % 8) * 2 + core, xl * 16 + ((z + 7) % 8) * 2 + core]
    greet([("blk", p) for p in ring + [across, sibling]])
    copies = []
    x_copy = send(w_ref, o_ref.at[xl, z, core], x_send, x_recv, "blk", across)

    def share(src, dst, e, i):
        copies.append(send(src, dst, c_send.at[e, i], c_recv.at[e, i], "blk", sibling))

    hops = [[4, 3], [3, 4]]
    travelling = {}
    for s in range(5):
        for e in range(2):
            x = xl if e == 0 else 1 - xl
            if s == 0:
                if e == 1:
                    x_copy.wait()
                here = o_ref.at[x, z, core]
                src = w_ref if e == 0 else here
                for d in range(2):
                    travelling[e, d] = send(
                        src, here, z_send.at[e, d, 0], z_recv.at[e, d, 0], "blk", ring[d]
                    )
                share(src, here, e, 0)
                continue
            for d in range(2):
                if s > hops[e][d]:
                    continue
                origin = (z + (8 - s)) % 8 if d == 0 else (z + s) % 8
                here = o_ref.at[x, origin, core]
                travelling[e, d].wait_recv()
                copies_done = travelling[e, d]
                copies.append((copies_done,))
                if s < hops[e][d]:
                    travelling[e, d] = send(
                        here, here, z_send.at[e, d, s], z_recv.at[e, d, s], "blk", ring[d]
                    )
                share(here, here, e, 4 * d + s)
    o_ref[xl, z, core] = w_ref[...]
    for copy in copies:
        if isinstance(copy, tuple):
            copy[0].wait_send()
        else:
            copy.wait()


def gather_rows(rows):
    scratch = [DMA((2, 2, 4)), DMA((2, 2, 4)), DMA, DMA, DMA((2, 9)), DMA((2, 9))]
    (out,) = call(gather_kernel, [(2, 8, 2, 32, 4 * W)], scratch, 1, [rows], 2**22)
    return out.reshape(1024, 4 * W)


def split(value):
    high = value.astype(jnp.bfloat16)
    return high, (value - high.astype(jnp.float32)).astype(jnp.bfloat16)


def tail_kernel(
    p_ref, u_ref, base_ref, o_ref, diag_ref, parent_ref,
    held, final, u_high, u_low, t_ref, pair, z_held, total, x_held, part, h_held, y_held,
    y_send, y_recv, x_send, x_recv, s_sem, r_sem,
):
    g, b = lax.axis_index("grp"), lax.axis_index("blk")
    y, h = g // 2, g % 2
    core, z, xl = b % 2, (b // 2) % 8, b // 16
    far_first = (4, 3, 5, 2, 6, 1, 7)
    sibling, across = xl * 16 + z * 2 + 1 - core, (1 - xl) * 16 + z * 2 + core
    z_peers = {d: xl * 16 + ((z + d) % 8) * 2 + core for d in far_first}
    y_peers = {d: ((y + d) % 8) * 2 + h for d in far_first}
    ring = [y_peers[1], y_peers[7]]
    other = y * 2 + 1 - h
    greet(
        [("blk", sibling), ("blk", across), ("grp", other)]
        + [("blk", z_peers[d]) for d in far_first]
        + [("grp", y_peers[d]) for d in far_first]
    )
    ring_copies = {}
    for s in range(8):
        for q in range(4):
            columns = pl.ds(q * W, W)
            chunk = (y + (7 - s)) % 8 if q % 2 == 0 else (y + 1 + s) % 8
            rows = pl.ds(pl.multiple_of(chunk * 64, 64), 64)
            if s == 0:
                src = p_ref.at[rows, columns]
            else:
                ring_copies[s - 1, q].wait_recv()
                held[s - 1, q] = held[s - 1, q] + p_ref[rows, columns]
                src = held.at[s - 1, q]
            if s < 7:
                ring_copies[s, q] = send(
                    src, held.at[s, q], y_send.at[s, q], y_recv.at[s, q], "grp", ring[q % 2]
                )
            else:
                theirs = pl.ds(pl.multiple_of((1 - h) * 32, 32), 32)
                ring_copies[s, q] = send(
                    held.at[6, q, theirs], final.at[q], x_send.at[q], x_recv.at[q], "grp", other
                )
        if s == 0:
            for q in range(4):
                u_high[q], u_low[q] = split(u_ref[:, q * W : (q + 1) * W].T)
    mine = pl.ds(pl.multiple_of(h * 32, 32), 32)
    for q in range(4):
        ring_copies[7, q].wait_recv()
        piece = held[6, q, mine] + final[q]
        o_ref[:, q * W : (q + 1) * W] = piece
        high, low = split(piece)

        def product(i):
            def mul(p, r):
                return jnp.dot(p[i], r, preferred_element_type=jnp.float32)

            return mul(u_high, low) + mul(u_low, high) + mul(u_high, high)

        diag = product(q)
        for j in range(8):
            t_ref[4 * (q % 2) + j // 2, j % 2, q // 2, :32] = diag[j * 32 : (j + 1) * 32]
        if q >= 2:
            mixed = product(q - 2)
            for j in range(16):
                t_ref[j // 2, j % 2, q - 2, 32:] = mixed[j * 16 : (j + 1) * 16]
    copies = []

    def pass_on(src, dst, i, axis, peer):
        copies.append(send(src, dst, s_sem.at[i], r_sem.at[i], axis, peer))
        return copies[-1]

    first = {}
    for d in far_first + (8,):
        k = (z + d) % 8
        first[d] = pass_on(t_ref.at[k, 1 - core], pair.at[k], 8 + d, "blk", sibling)
    second = {}
    for d in far_first:
        k = (z + d) % 8
        first[d].wait_recv()
        pair[k] = pair[k] + t_ref[k, core]
        second[d] = pass_on(pair.at[k], z_held.at[d - 1], d, "blk", z_peers[d])
    first[8].wait_recv()
    total[...] = pair[z] + t_ref[z, core]
    for d in reversed(far_first):
        second[d].wait_recv()
        total[...] = total[...] + z_held[d - 1]
    pass_on(total.at[1 - xl], x_held, 17, "blk", across).wait_recv()
    part[...] = total[xl] + x_held[...]
    pass_on(part, h_held, 18, "grp", other).wait_recv()
    y_held[y] = part[...] + h_held[...]
    third = [pass_on(y_held.at[y], y_held.at[y], 18 + d, "grp", y_peers[d]) for d in far_first]
    for copy in third:
        copy.wait_recv()
    result = y_held[0]
    for k in range(1, 8):
        result = result + y_held[k]
    result = result + base_ref[...]
    diag_ref[...] = result[:32]
    parent_ref[...] = -result[32:]
    for copy in copies + list(ring_copies.values()):
        copy.wait_send()


def scatter_and_sum(partial, w_own, base):
    f32, bf16 = jnp.float32, jnp.bfloat16
    scratch = [
        pltpu.VMEM((7, 4, 64, W), f32),
        pltpu.VMEM((4, 32, W), f32),
        pltpu.VMEM((4, W, 32), bf16),
        pltpu.VMEM((4, W, 32), bf16),
        pltpu.VMEM((8, 2, 2, 48, W), f32),
        pltpu.VMEM((8, 2, 48, W), f32),
        pltpu.VMEM((7, 2, 48, W), f32),
        pltpu.VMEM((2, 48, W), f32),
        pltpu.VMEM((48, W), f32),
        pltpu.VMEM((48, W), f32),
        pltpu.VMEM((48, W), f32),
        pltpu.VMEM((8, 48, W), f32),
        DMA((7, 4)),
        DMA((7, 4)),
        DMA((4,)),
        DMA((4,)),
        DMA((26,)),
        DMA((26,)),
    ]
    shapes = [(32, 4 * W), (32, W), (16, W)]
    return call(tail_kernel, shapes, scratch, 2, [partial, w_own, base], 2**23)


def per_device(sigma_anc, panels, diag_inv, scaled_parent_panel, struct_upper, struct_lower):
    grp = lax.axis_index("grp")
    blk = lax.axis_index("blk")
    v = [scaled_parent_panel[:W], scaled_parent_panel[W:]]
    u = panels * listed(struct_upper, struct_lower, (grp * 32 + blk) // 8)
    x = [dot(u[:, c * W : (c + 1) * W], v[c], 1, 0) - u[:, (c + 2) * W : (c + 3) * W] for c in (0, 1)]
    w = jnp.concatenate([u[:, : 2 * W], x[0], x[1]], axis=1)
    moves = [(q, (q % 16) * 32 + q // 16) for q in range(512)]
    w_own = lax.ppermute(w, ("grp", "blk"), moves)
    gathered = gather_rows(w)
    base_parent = [dot(diag_inv[c * W : (c + 1) * W], v[c], 1, 0, HIGHEST) for c in (0, 1)]
    base_low = [dot(v[c], base_parent[c], 0, 0, HIGHEST) for c in (0, 1)]
    zero = jnp.zeros((2 * W, W), jnp.float32)
    base_diag = diag_inv + jnp.concatenate([zero] + base_low, axis=0)
    base = jnp.concatenate(
        [
            lax.dynamic_slice_in_dim(base_diag, blk * 32, 32, 0),
            lax.dynamic_slice_in_dim(jnp.concatenate(base_parent, axis=0), blk * 16, 16, 0),
        ],
        axis=0,
    )
    partial = dot(sigma_anc, gathered, 0, 0)
    t, cov_diag, cov_parent = scatter_and_sum(partial, w_own, base)
    own = listed(struct_upper, struct_lower, (blk * 16 + grp) // 8)
    sign = jnp.where(jnp.arange(4 * W) < 2 * W, -1.0, 1.0).astype(jnp.float32)[None, :]
    cov_panel = t * (own * sign)
    return (cov_panel, cov_diag, cov_parent)


def solution(mesh):
    return jax.shard_map(
        per_device,
        mesh=mesh,
        in_specs=(P("grp", "blk"), P(("grp", "blk"), None), P(), P(), P(), P()),
        out_specs=(P(("blk", "grp"), None), P("blk", None), P("blk", None)),
        check_vma=False,
    )
```

```python
import jax
import jax.numpy as jnp
from jax import lax
from jax.experimental import pallas as pl
from jax.experimental.pallas import tpu as pltpu
from jax.sharding import PartitionSpec as P

W = 256
HIGH = lax.Precision.HIGH
HIGHEST = lax.Precision.HIGHEST


def dot(a, b, ca, cb, precision=HIGH):
    return lax.dot_general(
        a, b, (((ca,), (cb,)), ((), ())), precision=precision, preferred_element_type=jnp.float32
    )


def listed(struct_upper, struct_lower, block):
    upper = jnp.any(struct_upper == block, axis=1)
    lower = jnp.any(struct_lower == block, axis=1)
    flags = jnp.concatenate([upper, lower]).astype(jnp.float32)
    return jnp.repeat(flags, W)[None, :]


VMEM = pl.BlockSpec(memory_space=pltpu.VMEM)
DMA = pltpu.SemaphoreType.DMA


def greet(axes_and_peers):
    barrier = pltpu.get_barrier_semaphore()
    for axis, peer in axes_and_peers:
        pl.semaphore_signal(
            barrier, inc=1, device_id={axis: peer}, device_id_type=pl.DeviceIdType.MESH
        )
    pl.semaphore_wait(barrier, len(axes_and_peers))


def send(src, dst, send_sem, recv_sem, axis, peer):
    copy = pltpu.make_async_remote_copy(
        src_ref=src,
        dst_ref=dst,
        send_sem=send_sem,
        recv_sem=recv_sem,
        device_id={axis: peer},
        device_id_type=pl.DeviceIdType.MESH,
    )
    copy.start()
    return copy


def call(kernel, out_shapes, scratch, collective_id, operands, sent):
    return pl.pallas_call(
        kernel,
        out_shape=[jax.ShapeDtypeStruct(shape, jnp.float32) for shape in out_shapes],
        in_specs=[VMEM] * len(operands),
        out_specs=[VMEM] * len(out_shapes),
        scratch_shapes=scratch,
        cost_estimate=pl.CostEstimate(flops=1000000, bytes_accessed=sent, transcendentals=0),
        compiler_params=pltpu.CompilerParams(
            collective_id=collective_id, has_side_effects=True, vmem_limit_bytes=18 * 2**20
        ),
    )(*operands)


def gather_kernel(w_ref, o_ref, z_send, z_recv, x_send, x_recv, c_send, c_recv):
    b = lax.axis_index("blk")
    core, z, xl = b % 2, (b // 2) % 8, b // 16
    across, sibling = (1 - xl) * 16 + z * 2 + core, xl * 16 + z * 2 + 1 - core
    ring = [xl * 16 + ((z + 1) % 8) * 2 + core, xl * 16 + ((z + 7) % 8) * 2 + core]
    greet([("blk", p) for p in ring + [across, sibling]])
    copies = []
    x_copy = send(w_ref, o_ref.at[xl, z, core], x_send, x_recv, "blk", across)

    def share(src, dst, e, i):
        copies.append(send(src, dst, c_send.at[e, i], c_recv.at[e, i], "blk", sibling))

    hops = [[4, 3], [3, 4]]
    travelling = {}
    for s in range(5):
        for e in range(2):
            x = xl if e == 0 else 1 - xl
            if s == 0:
                if e == 1:
                    x_copy.wait()
                here = o_ref.at[x, z, core]
                src = w_ref if e == 0 else here
                for d in range(2):
                    travelling[e, d] = send(
                        src, here, z_send.at[e, d, 0], z_recv.at[e, d, 0], "blk", ring[d]
                    )
                share(src, here, e, 0)
                continue
            for d in range(2):
                if s > hops[e][d]:
                    continue
                origin = (z + (8 - s)) % 8 if d == 0 else (z + s) % 8
                here = o_ref.at[x, origin, core]
                travelling[e, d].wait_recv()
                copies_done = travelling[e, d]
                copies.append((copies_done,))
                if s < hops[e][d]:
                    travelling[e, d] = send(
                        here, here, z_send.at[e, d, s], z_recv.at[e, d, s], "blk", ring[d]
                    )
                share(here, here, e, 4 * d + s)
    o_ref[xl, z, core] = w_ref[...]
    for copy in copies:
        if isinstance(copy, tuple):
            copy[0].wait_send()
        else:
            copy.wait()


def gather_rows(rows):
    scratch = [DMA((2, 2, 4)), DMA((2, 2, 4)), DMA, DMA, DMA((2, 9)), DMA((2, 9))]
    (out,) = call(gather_kernel, [(2, 8, 2, 32, 4 * W)], scratch, 1, [rows], 2**22)
    return out.reshape(1024, 4 * W)


def split(value):
    high = value.astype(jnp.bfloat16)
    return high, (value - high.astype(jnp.float32)).astype(jnp.bfloat16)


def tail_kernel(
    p_ref, u_ref, base_ref, o_ref, diag_ref, parent_ref,
    held, final, u_high, u_low, t_ref, pair, z_held, total, x_held, part, h_held, y_held,
    y_send, y_recv, x_send, x_recv, s_sem, r_sem,
):
    g, b = lax.axis_index("grp"), lax.axis_index("blk")
    y, h = g // 2, g % 2
    core, z, xl = b % 2, (b // 2) % 8, b // 16
    far_first = (4, 3, 5, 2, 6, 1, 7)
    sibling, across = xl * 16 + z * 2 + 1 - core, (1 - xl) * 16 + z * 2 + core
    z_peers = {d: xl * 16 + ((z + d) % 8) * 2 + core for d in far_first}
    y_peers = {d: ((y + d) % 8) * 2 + h for d in far_first}
    ring = [y_peers[1], y_peers[7]]
    other = y * 2 + 1 - h
    greet(
        [("blk", sibling), ("blk", across), ("grp", other)]
        + [("blk", z_peers[d]) for d in far_first]
        + [("grp", y_peers[d]) for d in far_first]
    )
    ring_copies = {}
    for s in range(8):
        for q in range(4):
            columns = pl.ds(q * W, W)
            chunk = (y + (7 - s)) % 8 if q % 2 == 0 else (y + 1 + s) % 8
            rows = pl.ds(pl.multiple_of(chunk * 64, 64), 64)
            if s == 0:
                src = p_ref.at[rows, columns]
            else:
                ring_copies[s - 1, q].wait_recv()
                held[s - 1, q] = held[s - 1, q] + p_ref[rows, columns]
                src = held.at[s - 1, q]
            if s < 7:
                ring_copies[s, q] = send(
                    src, held.at[s, q], y_send.at[s, q], y_recv.at[s, q], "grp", ring[q % 2]
                )
            else:
                theirs = pl.ds(pl.multiple_of((1 - h) * 32, 32), 32)
                ring_copies[s, q] = send(
                    held.at[6, q, theirs], final.at[q], x_send.at[q], x_recv.at[q], "grp", other
                )
        if s == 0:
            for q in range(4):
                u_high[q], u_low[q] = split(u_ref[:, q * W : (q + 1) * W].T)
    mine = pl.ds(pl.multiple_of(h * 32, 32), 32)
    for q in range(4):
        ring_copies[7, q].wait_recv()
        piece = held[6, q, mine] + final[q]
        o_ref[:, q * W : (q + 1) * W] = piece
        high, low = split(piece)

        def product(i):
            def mul(p, r):
                return jnp.dot(p[i], r, preferred_element_type=jnp.float32)

            return mul(u_high, low) + mul(u_low, high) + mul(u_high, high)

        diag = product(q)
        for j in range(8):
            t_ref[4 * (q % 2) + j // 2, j % 2, q // 2, :32] = diag[j * 32 : (j + 1) * 32]
        if q >= 2:
            mixed = product(q - 2)
            for j in range(16):
                t_ref[j // 2, j % 2, q - 2, 32:] = mixed[j * 16 : (j + 1) * 16]
    copies = []

    def pass_on(src, dst, i, axis, peer):
        copies.append(send(src, dst, s_sem.at[i], r_sem.at[i], axis, peer))
        return copies[-1]

    first = {}
    for d in far_first + (8,):
        k = (z + d) % 8
        first[d] = pass_on(t_ref.at[k, 1 - core], pair.at[k], 8 + d, "blk", sibling)
    second = {}
    for d in far_first:
        k = (z + d) % 8
        first[d].wait_recv()
        pair[k] = pair[k] + t_ref[k, core]
        second[d] = pass_on(pair.at[k], z_held.at[d - 1], d, "blk", z_peers[d])
    first[8].wait_recv()
    total[...] = pair[z] + t_ref[z, core]
    for d in reversed(far_first):
        second[d].wait_recv()
        total[...] = total[...] + z_held[d - 1]
    pass_on(total.at[1 - xl], x_held, 17, "blk", across).wait_recv()
    part[...] = total[xl] + x_held[...]
    pass_on(part, h_held, 18, "grp", other).wait_recv()
    y_held[y] = part[...] + h_held[...]
    third = [pass_on(y_held.at[y], y_held.at[y], 18 + d, "grp", y_peers[d]) for d in far_first]
    for copy in third:
        copy.wait_recv()
    result = y_held[0]
    for k in range(1, 8):
        result = result + y_held[k]
    result = result + base_ref[...]
    diag_ref[...] = result[:32]
    parent_ref[...] = -result[32:]
    for copy in copies + list(ring_copies.values()):
        copy.wait_send()


def scatter_and_sum(partial, w_own, base):
    f32, bf16 = jnp.float32, jnp.bfloat16
    scratch = [
        pltpu.VMEM((7, 4, 64, W), f32),
        pltpu.VMEM((4, 32, W), f32),
        pltpu.VMEM((4, W, 32), bf16),
        pltpu.VMEM((4, W, 32), bf16),
        pltpu.VMEM((8, 2, 2, 48, W), f32),
        pltpu.VMEM((8, 2, 48, W), f32),
        pltpu.VMEM((7, 2, 48, W), f32),
        pltpu.VMEM((2, 48, W), f32),
        pltpu.VMEM((48, W), f32),
        pltpu.VMEM((48, W), f32),
        pltpu.VMEM((48, W), f32),
        pltpu.VMEM((8, 48, W), f32),
        DMA((7, 4)),
        DMA((7, 4)),
        DMA((4,)),
        DMA((4,)),
        DMA((26,)),
        DMA((26,)),
    ]
    shapes = [(32, 4 * W), (32, W), (16, W)]
    return call(tail_kernel, shapes, scratch, 2, [partial, w_own, base], 2**23)


def per_device(sigma_anc, panels, diag_inv, scaled_parent_panel, struct_upper, struct_lower):
    grp = lax.axis_index("grp")
    blk = lax.axis_index("blk")
    v = [scaled_parent_panel[:W], scaled_parent_panel[W:]]
    u = panels * listed(struct_upper, struct_lower, (grp * 32 + blk) // 8)
    x = [dot(u[:, c * W : (c + 1) * W], v[c], 1, 0) - u[:, (c + 2) * W : (c + 3) * W] for c in (0, 1)]
    w = jnp.concatenate([u[:, : 2 * W], x[0], x[1]], axis=1)
    moves = [(q, (q % 16) * 32 + q // 16) for q in range(512)]
    w_own = lax.ppermute(w, ("grp", "blk"), moves)
    def rows_of(a, first, count):
        return lax.dynamic_slice_in_dim(a, first, count, 0)

    pair = rows_of(diag_inv, blk * 16, 16)
    base_parent = dot(pair, rows_of(scaled_parent_panel, (blk // 16) * W, W), 1, 0, HIGHEST)
    lower = jnp.maximum(blk - 16, 0)
    v_low = rows_of(scaled_parent_panel, (lower // 8) * W, W)
    v_some = lax.dynamic_slice_in_dim(v_low, (lower % 8) * 32, 32, 1)
    left = dot(v_some, rows_of(diag_inv, (lower // 8) * W, W), 0, 0, HIGHEST)
    base_low = jnp.where(blk >= 16, dot(left, v_low, 1, 0, HIGHEST), 0.0)
    base = jnp.concatenate([rows_of(diag_inv, blk * 32, 32) + base_low, base_parent], axis=0)
    w, base = lax.optimization_barrier((w, base))
    gathered = gather_rows(w)
    partial = dot(sigma_anc, gathered, 0, 0)
    t, cov_diag, cov_parent = scatter_and_sum(partial, w_own, base)
    own = listed(struct_upper, struct_lower, (blk * 16 + grp) // 8)
    sign = jnp.where(jnp.arange(4 * W) < 2 * W, -1.0, 1.0).astype(jnp.float32)[None, :]
    cov_panel = t * (own * sign)
    return (cov_panel, cov_diag, cov_parent)


def solution(mesh):
    return jax.shard_map(
        per_device,
        mesh=mesh,
        in_specs=(P("grp", "blk"), P(("grp", "blk"), None), P(), P(), P(), P()),
        out_specs=(P(("blk", "grp"), None), P("blk", None), P("blk", None)),
        check_vma=False,
    )
```
